32 devices in a mesh: blk: 16 (over z, x, core), narrow: 2 (over y).
Axes of the slice: x: 2, y: 2, z: 4, core: 2. Of those that a mesh axis runs over, the one named last changes fastest.
Arguments:
- rhs: float32 [6144, 256], P('blk', 'narrow'), may hold values from -6 to 6
- zo: float32 [6144, 64], P('blk'), may hold values from -0.109375 to 0.109375
- e_diag: float32 [64, 96, 96], P('blk'), may hold values from -0.18 to 0.18
- a_off: float32 [64, 3, 96, 96], P('blk'), may hold values from -0.18 to 0.18
- e_off: float32 [64, 3, 96, 96], P('blk'), may hold values from -0.09 to 0.09
- col_index: int32 [64, 3], P('blk'), may hold values from 0 to 63, as said below
- inv_diag: float32 [2, 64, 96, 96], P(None, 'blk'), may hold values from -0.625 to 0.625
- shifts: float32 [2], replicated, may hold values from 0.5 to 2
Outputs:
- residual: float32 [6144, 256], P('blk', 'narrow')
- cross: float32 [64, 2, 256], P(('blk', 'narrow'))
The draws below stay inside these ranges and needn't reach their ends.
Inputs may be any that keep to these rules, and one draw needn't show every extreme that they name: `col_index`: each block column index differs from its own block row by 1 or 2 in either direction, near the ends of the range reflected to the other side; the three indices of a row may repeat.
All inputs are finite; a program needn't handle non-finite values.
Results may differ from the reference program's by a relative error of at most 0.0001.
Values sent between devices are 32-bit elements; how exact they have to be, the bound alone decides.
A program may use at most 64 MiB of HBM per device.

```python
import math
import jax
import jax.numpy as jnp
from jax import lax

BD = 96
CPL = 3
SWEEPS = 8
NB = 64
NN = 6144
K = 256
KO = 64


def draw_col_index(key, part):
    block_rows = jnp.arange(NB, dtype=jnp.int32)
    dropped = jax.random.randint(key, (NB,), 0, 4).astype(jnp.int32)
    dropped = jnp.where(block_rows == NB - 2, 0, dropped)
    dropped = jnp.where(block_rows == 1, 3, dropped)
    offsets = jnp.array([-2, -1, 1, 2], jnp.int32)
    slots = jnp.arange(3, dtype=jnp.int32)[None, :]
    picks = slots + (slots >= dropped[:, None]).astype(jnp.int32)
    chosen = offsets[picks]
    columns = block_rows[:, None] + chosen
    outside = (columns < 0) | (columns >= NB)
    return jnp.where(outside, block_rows[:, None] - chosen, columns).astype(jnp.int32)


def strengthened(result, stream_key, source, target, parts, factor):
    owner, partner = [(jnp.arange(result.shape[position]) // (result.shape[position] // parts)).reshape([-1 if axis == position else 1 for axis in range(result.ndim)]) for position in (source, target)]
    chosen = jax.random.permutation(stream_key, parts)[partner]
    strong = (owner == chosen) | (owner == (partner + parts // 2) % parts)
    return jnp.where(strong, factor * result, result)


def shard_levels(own_key, shape, cuts, least, largest):
    gain, own = 1.0, jax.random.fold_in(own_key, 6)
    for position, shards_of in cuts:
        steps = jnp.exp(jax.random.uniform(jax.random.fold_in(own, position), (shards_of,), jnp.float32, least / len(cuts), largest / len(cuts)))
        gain = gain * jnp.repeat(steps, shape[position] // shards_of).reshape([-1 if axis == position else 1 for axis in range(len(shape))])
    return gain


def centred(stream_key, shape, deviation, most, split=(), held_as=jnp.bfloat16):
    values = deviation * jax.random.normal(stream_key, shape, jnp.float32)
    if split:
        values = values * shard_levels(stream_key, shape, split, -0.22, 0.18)
    return jnp.clip(values, -most, most).astype(held_as)


def bell_draw_with(key, shape, spread, reach, shards, heavy, kind=jnp.bfloat16):
    drawn = spread * jax.random.normal(key, shape, jnp.float32)
    if shards:
        drawn = drawn * shard_levels(key, shape, shards, -0.22, 0.18)
    return jnp.clip(strengthened(drawn, jax.random.fold_in(key, 3), *heavy), -reach, reach).astype(kind)


def setup_inputs(seed: int = 0) -> dict:
    arg_keys = jax.random.split(jax.random.key(seed), 9)
    return {
        "rhs": centred(arg_keys[0], (NN, K), 1.0, 6.0, ((0, 16), (1, 2)), jnp.float32),
        "zo": bell_draw_with(arg_keys[1], (NN, KO), NN ** -0.5, 0.109375, ((0, 16),), (0, 1, 16, 2.0), jnp.float32),
        "e_diag": centred(arg_keys[2], (NB, BD, BD), 0.0306, 0.18, ((0, 16),), jnp.float32),
        "a_off": centred(arg_keys[3], (NB, CPL, BD, BD), 0.0306, 0.18, ((0, 16),), jnp.float32),
        "e_off": centred(arg_keys[4], (NB, CPL, BD, BD), 0.0153, 0.09, ((0, 16),), jnp.float32),
        "col_index": draw_col_index(jax.random.fold_in(arg_keys[8], 71), 0),
        "inv_diag": centred(arg_keys[6], (2, NB, BD, BD), BD ** -0.5, 0.625, ((1, 16),), jnp.float32),
        "shifts": jnp.clip(jnp.exp(jax.random.uniform(arg_keys[7], (2,), jnp.float32, math.log(0.5), math.log(2.0))), 0.5, 2.0),
    }


precise = lax.Precision.HIGHEST

def block_product(matrices, field):
    return jnp.einsum('nab,nbk->nak', matrices, field, precision=precise)

def coupled_product(coupling, col_index, field):
    picked = jnp.take(field, col_index, axis=0)
    return jnp.einsum('nsab,nsbk->nak', coupling, picked, precision=precise)

def reference(rhs, zo, e_diag, a_off, e_off, col_index, inv_diag, shifts):
    columns = rhs.shape[1]
    current = rhs.reshape(NB, BD, columns)
    images = []
    for which in range(2):
        shift_value = shifts[which]
        coupling = a_off - shift_value * e_off
        inverse = inv_diag[which]
        iterate = block_product(inverse, current)
        for sweep in range(SWEEPS):
            iterate = block_product(inverse, current - coupled_product(coupling, col_index, iterate))
        mass_image = block_product(e_diag, iterate) + coupled_product(e_off, col_index, iterate)
        current = current + 2.0 * shift_value * mass_image
        images.append(jnp.sqrt(2.0 * shift_value) * mass_image)
    stacked = jnp.stack(images, axis=2).reshape(NN, 2, columns)
    cross = jnp.einsum('ro,rsk->osk', zo, stacked, precision=precise)
    return (current.reshape(NN, columns), cross)
```

```python
import functools

import jax
import jax.numpy as jnp
from jax import lax
from jax.experimental import pallas as pl
from jax.experimental.pallas import tpu as pltpu
from jax.sharding import PartitionSpec as P

SWEEPS = 8
SLOTS = 2 * (SWEEPS + 1)
OFFSETS = (-2, -1, 1, 2)
LANES = 128
E_MATRIX = 2
f32, bf16 = jnp.float32, jnp.bfloat16
NEAR, FAR = 0, 1


def split(x):
    high = x.astype(bf16)
    return high, (x - high.astype(f32)).astype(bf16)


def beside(x):
    return jnp.concatenate(split(x), axis=1)


def below(x):
    return jnp.concatenate(split(x), axis=0)


def product(matrix, field):
    whole = jnp.dot(matrix, field, preferred_element_type=f32)
    rows, cols = whole.shape[0] // 2, whole.shape[1] // 2
    return (whole[:rows, :cols] + whole[:rows, cols:]) + (whole[rows:, :cols] + whole[rows:, cols:])


def kernel(
    count, others, size,
    rhs_ref, zo_ref, e_diag_ref, a_off_ref, e_off_ref, col_ref, inv_ref, shift_ref,
    res_ref, cross_ref,
    own, halo, pend, base, image, band, diag, local_m, halo_m, inverse, zot, partial, outbox, inbox,
    send_sem, recv_sem, cross_send, cross_recv,
):
    me = lax.axis_index("blk")
    mine = lax.axis_index("narrow")
    devices = count * others
    rank = me * others + mine
    parity = lax.rem(me, 2)
    halves = (1 - parity, parity)
    step_to = 1 - 2 * parity
    has_far = jnp.logical_and(me != 0, me != count - 1)
    near_id = me + step_to
    far_id = jnp.where(has_far, me - step_to, near_id)
    half_rows = 2 * size
    per = outbox.shape[2]

    barrier = pltpu.get_barrier_semaphore()

    def greet(d, carry):
        @pl.when(d != rank)
        def _():
            pl.semaphore_signal(
                barrier, inc=1,
                device_id={"blk": d // others, "narrow": lax.rem(d, others)},
                device_id_type=pl.DeviceIdType.MESH,
            )
        return carry

    lax.fori_loop(0, devices, greet, 0)

    @pl.when(jnp.logical_not(has_far))
    def _():
        def clear(s, carry):
            halo[s, FAR] = jnp.zeros((half_rows, LANES), f32)
            return carry
        lax.fori_loop(0, SLOTS, clear, 0)

    def copy_of(slot, side):
        return pltpu.make_async_remote_copy(
            src_ref=own.at[slot, halves[side]],
            dst_ref=halo.at[slot, side],
            send_sem=send_sem.at[slot, side],
            recv_sem=recv_sem.at[slot, side],
            device_id={"blk": near_id if side == NEAR else far_id},
            device_id_type=pl.DeviceIdType.MESH,
        )

    def send(slot, side):
        if side == NEAR:
            copy_of(slot, side).start()
        else:
            @pl.when(has_far)
            def _():
                copy_of(slot, side).start()

    def arrive(slot, side):
        if side == NEAR:
            copy_of(slot, side).wait_recv()
        else:
            @pl.when(has_far)
            def _():
                copy_of(slot, side).wait_recv()

    filler = jnp.zeros((LANES - size, 2 * LANES), bf16)

    def field(pieces):
        parts = []
        for piece in pieces:
            for b in range(2):
                parts += [beside(piece[b * size:(b + 1) * size]), filler]
        return jnp.concatenate(parts, axis=0)

    def solved(which, half, value):
        return jnp.concatenate(
            [product(inverse[which, half * 2 + b], beside(value[b * size:(b + 1) * size])) for b in range(2)], axis=0
        )

    def place(which, row, blocks):
        empty = jnp.zeros((size, LANES), bf16)
        half = row // 2
        for c in range(-2, 6):
            high, low = split(blocks[c - row]) if c - row in blocks else (empty, empty)
            if 0 <= c < 4:
                lanes = slice(c * LANES, (c + 1) * LANES)
                local_m[which, row * size:(row + 1) * size, lanes] = high
                local_m[which, (4 + row) * size:(5 + row) * size, lanes] = low
            elif (c < 0) == (half == 0):
                k = c + 2 if c < 0 else c - 4
                at = row - 2 * half
                lanes = slice(k * LANES, (k + 1) * LANES)
                halo_m[which, half, at * size:(at + 1) * size, lanes] = high
                halo_m[which, half, (2 + at) * size:(3 + at) * size, lanes] = low

    def build_bands():
        band[...] = jnp.zeros_like(band)
        diag[...] = jnp.zeros_like(diag)
        for i in range(4):
            diag[i, :, 0:size] = e_diag_ref[i]
            for k, offset in enumerate(OFFSETS):
                total_a = jnp.zeros((size, size), f32)
                total_e = jnp.zeros((size, size), f32)
                for s in range(3):
                    weight = jnp.where(col_ref[i, s] == me * 4 + (i + offset), f32(1.0), f32(0.0))
                    total_a = total_a + weight * a_off_ref[i, s]
                    total_e = total_e + weight * e_off_ref[i, s]
                band[0, i, :, k * LANES:k * LANES + size] = total_a
                band[1, i, :, k * LANES:k * LANES + size] = total_e

    def build_sweep(which):
        q = shift_ref[which]
        for i in range(4):
            merged = product(inverse[which, i], beside(band[0, i] - q * band[1, i]))
            place(which, i, {o: merged[:, k * LANES:(k + 1) * LANES] for k, o in enumerate(OFFSETS)})

    def build_mass():
        for i in range(4):
            blocks = {o: band[1, i, :, k * LANES:(k + 1) * LANES] for k, o in enumerate(OFFSETS)}
            blocks[0] = diag[i]
            place(E_MATRIX, i, blocks)

    def inner(which, slot):
        return product(local_m[which], field([own[slot, 0], own[slot, 1]]))

    def outer(which, slot, side):
        arrive(slot, side)
        return product(halo_m[which, halves[side]], field([halo[slot, side]]))

    def sweep_inner(which, slot):
        got = inner(which, slot)
        for half in range(2):
            pend[half] = base[half] - got[half * half_rows:(half + 1) * half_rows]

    def sweep_outer(which, slot):
        for side in (NEAR, FAR):
            own[slot + 1, halves[side]] = pend[halves[side]] - outer(which, slot, side)
            send(slot + 1, side)

    for which in range(2):
        for i in range(4):
            inverse[which, i] = below(inv_ref[which, i])
    for half in range(2):
        value = rhs_ref[half * half_rows:(half + 1) * half_rows]
        start = solved(0, half, value)
        base[half] = start
        own[0, half] = start
    pl.semaphore_wait(barrier, devices - 1)
    send(0, FAR)
    send(0, NEAR)
    build_bands()
    build_sweep(0)

    ko = zo_ref.shape[1]
    for which in range(2):
        first = which * (SWEEPS + 1)
        q = shift_ref[which]
        sweep_inner(which, first)
        sweep_outer(which, first)
        done = 1
        if which == 0:
            sweep_inner(which, first + 1)
            build_mass()
            sweep_outer(which, first + 1)
            sweep_inner(which, first + 2)
            build_sweep(1)
            sweep_outer(which, first + 2)
            zot[...] = below(jnp.transpose(zo_ref[...]))
            done = 3

        def sweep(s, carry):
            sweep_inner(which, first + s)
            sweep_outer(which, first + s)
            return carry

        lax.fori_loop(done, SWEEPS, sweep, 0)

        last = first + SWEEPS
        got = inner(E_MATRIX, last)
        for half in range(2):
            pend[half] = got[half * half_rows:(half + 1) * half_rows]
        root = jnp.sqrt(jnp.full((1, LANES), 2.0 * q, f32))
        for side in (NEAR, FAR):
            half = halves[side]
            mass = pend[half] + outer(E_MATRIX, last, side)
            rows = pl.ds(pl.multiple_of(half * half_rows, 8), half_rows)
            before = rhs_ref[rows, :] if which == 0 else res_ref[rows, :]
            after = before + (2.0 * q) * mass
            res_ref[rows, :] = after
            image[half] = root * mass
            if which == 0:
                start = solved(1, half, after)
                base[half] = start
                own[last + 1, half] = start
                send(last + 1, side)

        pieces = jnp.concatenate([beside(image[0]), beside(image[1])], axis=0)
        partial[...] = product(zot[...], pieces)

        def pack(d, carry):
            outbox[which, d] = partial[pl.ds(d * per, per), :]
            return carry

        lax.fori_loop(0, devices, pack, 0)

        def post(d, carry):
            @pl.when(d != rank)
            def _():
                pltpu.make_async_remote_copy(
                    src_ref=outbox.at[which, d],
                    dst_ref=inbox.at[which, rank],
                    send_sem=cross_send.at[which],
                    recv_sem=cross_recv.at[which],
                    device_id={"blk": d // others, "narrow": lax.rem(d, others)},
                    device_id_type=pl.DeviceIdType.MESH,
                ).start()
            return carry

        lax.fori_loop(0, devices, post, 0)
        inbox[which, rank] = outbox[which, rank]

    for which in range(2):
        most = pl.ds(0, devices - 1)
        pltpu.make_async_copy(outbox.at[which, most], inbox.at[which, most], cross_recv.at[which]).wait()
        for n in range(others):
            total = inbox[which, n]
            for b in range(1, count):
                total = total + inbox[which, b * others + n]
            cross_ref[:, which, n * LANES:(n + 1) * LANES] = total
        pltpu.make_async_copy(outbox.at[which, most], inbox.at[which, most], cross_send.at[which]).wait()

    def settle(slot, carry):
        copy_of(slot, NEAR).wait_send()

        @pl.when(has_far)
        def _():
            copy_of(slot, FAR).wait_send()
        return carry

    lax.fori_loop(0, SLOTS, settle, 0)


def shards(count, others, rhs, zo, e_diag, a_off, e_off, col_index, inv_diag, shifts):
    row_count, col_width = rhs.shape
    size = e_diag.shape[1]
    ko = zo.shape[1]
    devices = count * others
    per = ko // devices
    half_rows = 2 * size
    assert row_count == 4 * size and col_width == LANES and count % 2 == 0
    vmem = pl.BlockSpec(memory_space=pltpu.VMEM)
    smem = pl.BlockSpec(memory_space=pltpu.SMEM)
    return pl.pallas_call(
        functools.partial(kernel, count, others, size),
        out_shape=(
            jax.ShapeDtypeStruct((row_count, col_width), f32),
            jax.ShapeDtypeStruct((per, 2, others * LANES), f32),
        ),
        in_specs=[vmem, vmem, vmem, vmem, vmem, smem, vmem, smem],
        out_specs=(vmem, vmem),
        scratch_shapes=[
            pltpu.VMEM((SLOTS, 2, half_rows, LANES), f32),
            pltpu.VMEM((SLOTS, 2, half_rows, LANES), f32),
            pltpu.VMEM((2, half_rows, LANES), f32),
            pltpu.VMEM((2, half_rows, LANES), f32),
            pltpu.VMEM((2, half_rows, LANES), f32),
            pltpu.VMEM((2, 4, size, 4 * LANES), f32),
            pltpu.VMEM((4, size, LANES), f32),
            pltpu.VMEM((3, 8 * size, 4 * LANES), bf16),
            pltpu.VMEM((3, 2, 4 * size, 2 * LANES), bf16),
            pltpu.VMEM((2, 4, 2 * size, size), bf16),
            pltpu.VMEM((2 * ko, row_count), bf16),
            pltpu.VMEM((ko, LANES), f32),
            pltpu.VMEM((2, devices, per, LANES), f32),
            pltpu.VMEM((2, devices, per, LANES), f32),
            pltpu.SemaphoreType.DMA((SLOTS, 2)),
            pltpu.SemaphoreType.DMA((SLOTS, 2)),
            pltpu.SemaphoreType.DMA((2,)),
            pltpu.SemaphoreType.DMA((2,)),
        ],
        compiler_params=pltpu.CompilerParams(collective_id=0, has_side_effects=True),
    )(rhs, zo, e_diag, a_off, e_off, col_index, inv_diag, shifts)


def solution(mesh):
    placed = (
        P("blk", "narrow"),
        P("blk", None),
        P("blk", None, None),
        P("blk", None, None, None),
        P("blk", None, None, None),
        P("blk", None),
        P(None, "blk", None, None),
        P(),
    )
    return jax.shard_map(
        functools.partial(shards, mesh.shape["blk"], mesh.shape["narrow"]),
        mesh=mesh,
        in_specs=placed,
        out_specs=(P("blk", "narrow"), P(("blk", "narrow"), None, None)),
        check_vma=False,
    )
```

```python
import functools

import jax
import jax.numpy as jnp
from jax import lax
from jax.experimental import pallas as pl
from jax.experimental.pallas import tpu as pltpu
from jax.sharding import PartitionSpec as P

SWEEPS = 8
SLOTS = 2 * (SWEEPS + 1)
OFFSETS = (-2, -1, 1, 2)
LANES = 128
E_MATRIX = 2
f32, bf16 = jnp.float32, jnp.bfloat16
NEAR, FAR = 0, 1
EDGE, INNER = 0, 1


def split(x):
    high = x.astype(bf16)
    return high, (x - high.astype(f32)).astype(bf16)


def beside(x):
    return jnp.concatenate(split(x), axis=1)


def below(x):
    return jnp.concatenate(split(x), axis=0)


def product(matrix, field):
    whole = jnp.dot(matrix, field, preferred_element_type=f32)
    rows, cols = whole.shape[0] // 2, whole.shape[1] // 2
    return (whole[:rows, :cols] + whole[:rows, cols:]) + (whole[rows:, :cols] + whole[rows:, cols:])


def kernel(
    count, others, size,
    rhs_ref, zo_ref, e_diag_ref, a_off_ref, e_off_ref, col_ref, inv_ref, shift_ref,
    res_ref, cross_ref,
    own, halo, pend, base, image, band, diag, local_m, halo_m, inverse, zot, partial, outbox, inbox,
    send_sem, recv_sem, cross_send, cross_recv, tokens,
):
    me = lax.axis_index("blk")
    mine = lax.axis_index("narrow")
    devices = count * others
    rank = me * others + mine
    parity = lax.rem(me, 2)
    halves = (1 - parity, parity)
    step_to = 1 - 2 * parity
    has_far = jnp.logical_and(me != 0, me != count - 1)
    near_id = me + step_to
    far_id = jnp.where(has_far, me - step_to, near_id)
    per = outbox.shape[2]

    barrier = pltpu.get_barrier_semaphore()

    short = count <= SLOTS - 1

    def greet(**where):
        pl.semaphore_signal(barrier, inc=1, device_id=where, device_id_type=pl.DeviceIdType.MESH)

    def everyone(act):
        def at(b, carry):
            for n in range(others):
                @pl.when(jnp.logical_or(b != me, n != mine))
                def _():
                    act(b, n)
            return carry
        lax.fori_loop(0, count, at, 0)

    if short:
        greet(blk=near_id)

        @pl.when(has_far)
        def _():
            greet(blk=far_id)

        for k in range(1, others):
            greet(narrow=lax.rem(mine + k, others))
        greeted = others + jnp.where(has_far, 1, 0)
    else:
        everyone(lambda b, n: greet(blk=b, narrow=n))
        greeted = devices - 1

    @pl.when(jnp.logical_not(has_far))
    def _():
        def clear(s, carry):
            halo[s, FAR] = jnp.zeros((2, size, LANES), f32)
            return carry
        lax.fori_loop(0, SLOTS, clear, 0)

    def block_of(side, piece):
        return 3 * halves[side] if piece == EDGE else 1 + halves[side]

    def copy_of(slot, side, piece):
        return pltpu.make_async_remote_copy(
            src_ref=own.at[slot, block_of(side, piece)],
            dst_ref=halo.at[slot, side, piece],
            send_sem=send_sem.at[slot, side, piece],
            recv_sem=recv_sem.at[slot, side, piece],
            device_id={"blk": near_id if side == NEAR else far_id},
            device_id_type=pl.DeviceIdType.MESH,
        )

    def where_linked(side, act):
        if side == NEAR:
            act()
        else:
            pl.when(has_far)(act)

    def send(slot, side, piece):
        where_linked(side, lambda: copy_of(slot, side, piece).start())

    def arrive(slot, side, piece):
        where_linked(side, lambda: copy_of(slot, side, piece).wait_recv())

    filler = jnp.zeros((LANES - size, 2 * LANES), bf16)

    def field(blocks):
        parts = []
        for block in blocks:
            parts += [beside(block), filler]
        return jnp.concatenate(parts, axis=0)

    def solved(which, block, value):
        return product(inverse[which, block], beside(value))

    def place(which, row, blocks):
        empty = jnp.zeros((size, LANES), bf16)
        half = row // 2
        for c in range(-2, 6):
            high, low = split(blocks[c - row]) if c - row in blocks else (empty, empty)
            if 0 <= c < 4:
                lanes = slice(c * LANES, (c + 1) * LANES)
                local_m[which, row * size:(row + 1) * size, lanes] = high
                local_m[which, (4 + row) * size:(5 + row) * size, lanes] = low
            elif (c < 0) == (half == 0):
                k = EDGE if c in (-1, 4) else INNER
                at = EDGE if row in (0, 3) else INNER
                lanes = slice(k * LANES, (k + 1) * LANES)
                halo_m[which, half, 2 * at * size:(2 * at + 1) * size, lanes] = high
                halo_m[which, half, (2 * at + 1) * size:(2 * at + 2) * size, lanes] = low

    def build_bands():
        band[...] = jnp.zeros_like(band)
        diag[...] = jnp.zeros_like(diag)
        for i in range(4):
            diag[i, :, 0:size] = e_diag_ref[i]
            for k, offset in enumerate(OFFSETS):
                total_a = jnp.zeros((size, size), f32)
                total_e = jnp.zeros((size, size), f32)
                for s in range(3):
                    weight = jnp.where(col_ref[i, s] == me * 4 + (i + offset), f32(1.0), f32(0.0))
                    total_a = total_a + weight * a_off_ref[i, s]
                    total_e = total_e + weight * e_off_ref[i, s]
                band[0, i, :, k * LANES:k * LANES + size] = total_a
                band[1, i, :, k * LANES:k * LANES + size] = total_e

    def build_sweep(which):
        q = shift_ref[which]
        for i in range(4):
            merged = product(inverse[which, i], beside(band[0, i] - q * band[1, i]))
            place(which, i, {o: merged[:, k * LANES:(k + 1) * LANES] for k, o in enumerate(OFFSETS)})

    def build_mass():
        for i in range(4):
            blocks = {o: band[1, i, :, k * LANES:(k + 1) * LANES] for k, o in enumerate(OFFSETS)}
            blocks[0] = diag[i]
            place(E_MATRIX, i, blocks)

    def inner(which, slot):
        return product(local_m[which], field([own[slot, b] for b in range(4)]))

    def outer(which, slot, side, emit):
        part = 2 * size
        arrive(slot, side, EDGE)
        nearest = field([halo[slot, side, EDGE]])
        matrix = halo_m.at[which, halves[side]]
        emit(block_of(side, INNER), INNER, product(matrix[part:2 * part, 0:LANES], nearest))
        edge = product(matrix[0:part, 0:LANES], nearest)
        arrive(slot, side, INNER)
        edge = edge + product(matrix[0:part, LANES:2 * LANES], field([halo[slot, side, INNER]]))
        emit(block_of(side, EDGE), EDGE, edge)

    def pass_token(token, turn, target, slot):
        @pl.when(jnp.logical_and(turn == slot, turn > 0))
        def _():
            pl.semaphore_wait(tokens.at[token], 1)

        @pl.when(jnp.logical_and(turn == slot, turn < count - 1))
        def _():
            pl.semaphore_signal(
                tokens.at[token], inc=1, device_id={"blk": target}, device_id_type=pl.DeviceIdType.MESH
            )

    def pass_tokens(slot):
        if short:
            pass_token(0, me, jnp.minimum(me + 1, count - 1), slot)
            pass_token(1, count - 1 - me, jnp.maximum(me - 1, 0), slot)

    def sweep_inner(which, slot):
        pass_tokens(slot)
        got = inner(which, slot)
        for b in range(4):
            pend[b] = base[b] - got[b * size:(b + 1) * size]

    def sweep_outer(which, slot):
        for side in (NEAR, FAR):
            def emit(block, piece, value):
                own[slot + 1, block] = pend[block] - value
                send(slot + 1, side, piece)

            outer(which, slot, side, emit)

    for which in range(2):
        for i in range(4):
            inverse[which, i] = below(inv_ref[which, i])
    for b in range(4):
        start = solved(0, b, rhs_ref[b * size:(b + 1) * size])
        base[b] = start
        own[0, b] = start
    pl.semaphore_wait(barrier, greeted)
    for side in (FAR, NEAR):
        for piece in (EDGE, INNER):
            send(0, side, piece)
    build_bands()
    build_sweep(0)

    def post(which):
        def act(b, n):
            pltpu.make_async_remote_copy(
                src_ref=outbox.at[which, b * others + n],
                dst_ref=inbox.at[which, rank],
                send_sem=cross_send.at[which],
                recv_sem=cross_recv.at[which],
                device_id={"blk": b, "narrow": n},
                device_id_type=pl.DeviceIdType.MESH,
            ).start()

        everyone(act)

    for which in range(2):
        first = which * (SWEEPS + 1)
        q = shift_ref[which]
        sweep_inner(which, first)
        sweep_outer(which, first)
        done = 1
        if which == 0:
            sweep_inner(which, first + 1)
            build_mass()
            sweep_outer(which, first + 1)
            sweep_inner(which, first + 2)
            build_sweep(1)
            sweep_outer(which, first + 2)
            zot[...] = below(zo_ref[...])
            done = 3

        def sweep(s, carry):
            sweep_inner(which, first + s)
            sweep_outer(which, first + s)
            return carry

        lax.fori_loop(done, SWEEPS - which, sweep, 0)
        if which == 1:
            sweep_inner(which, first + SWEEPS - 1)
            post(0)
            sweep_outer(which, first + SWEEPS - 1)

        last = first + SWEEPS
        if which == 0:
            pass_tokens(last)
        got = inner(E_MATRIX, last)
        for b in range(4):
            pend[b] = got[b * size:(b + 1) * size]
        root = jnp.sqrt(jnp.full((1, LANES), 2.0 * q, f32))
        for side in (NEAR, FAR):
            def emit(block, piece, value):
                mass = pend[block] + value
                rows = pl.ds(pl.multiple_of(block * size, 8), size)
                before = rhs_ref[rows, :] if which == 0 else res_ref[rows, :]
                after = before + (2.0 * q) * mass
                res_ref[rows, :] = after
                image[block] = root * mass
                if which == 0:
                    start = solved(1, block, after)
                    base[block] = start
                    own[last + 1, block] = start
                    send(last + 1, side, piece)

            outer(E_MATRIX, last, side, emit)

        partial[...] = product(zot[...], jnp.concatenate([beside(image[b]) for b in range(4)], axis=0))

        def pack(d, carry):
            outbox[which, d] = partial[pl.ds(d * per, per), :]
            return carry

        lax.fori_loop(0, devices, pack, 0)

        if which == 1:
            post(1)
        inbox[which, rank] = outbox[which, rank]

    for which in range(2):
        most = pl.ds(0, devices - 1)
        pltpu.make_async_copy(outbox.at[which, most], inbox.at[which, most], cross_recv.at[which]).wait()
        for n in range(others):
            total = inbox[which, n]
            for b in range(1, count):
                total = total + inbox[which, b * others + n]
            cross_ref[:, which, n * LANES:(n + 1) * LANES] = total
        pltpu.make_async_copy(outbox.at[which, most], inbox.at[which, most], cross_send.at[which]).wait()

    def settle(slot, carry):
        for side in (NEAR, FAR):
            for piece in (EDGE, INNER):
                where_linked(side, lambda: copy_of(slot, side, piece).wait_send())
        return carry

    lax.fori_loop(0, SLOTS, settle, 0)


def shards(count, others, rhs, zo, e_diag, a_off, e_off, col_index, inv_diag, shifts):
    row_count, col_width = rhs.shape
    size = e_diag.shape[1]
    ko = zo.shape[1]
    devices = count * others
    per = ko // devices
    assert row_count == 4 * size and col_width == LANES and count % 2 == 0
    vmem = pl.BlockSpec(memory_space=pltpu.VMEM)
    smem = pl.BlockSpec(memory_space=pltpu.SMEM)
    return pl.pallas_call(
        functools.partial(kernel, count, others, size),
        out_shape=(
            jax.ShapeDtypeStruct((row_count, col_width), f32),
            jax.ShapeDtypeStruct((per, 2, others * LANES), f32),
        ),
        in_specs=[vmem, vmem, vmem, vmem, vmem, smem, vmem, smem],
        out_specs=(vmem, vmem),
        scratch_shapes=[
            pltpu.VMEM((SLOTS, 4, size, LANES), f32),
            pltpu.VMEM((SLOTS, 2, 2, size, LANES), f32),
            pltpu.VMEM((4, size, LANES), f32),
            pltpu.VMEM((4, size, LANES), f32),
            pltpu.VMEM((4, size, LANES), f32),
            pltpu.VMEM((2, 4, size, 4 * LANES), f32),
            pltpu.VMEM((4, size, LANES), f32),
            pltpu.VMEM((3, 8 * size, 4 * LANES), bf16),
            pltpu.VMEM((3, 2, 4 * size, 2 * LANES), bf16),
            pltpu.VMEM((2, 4, 2 * size, size), bf16),
            pltpu.VMEM((2 * ko, row_count), bf16),
            pltpu.VMEM((ko, LANES), f32),
            pltpu.VMEM((2, devices, per, LANES), f32),
            pltpu.VMEM((2, devices, per, LANES), f32),
            pltpu.SemaphoreType.DMA((SLOTS, 2, 2)),
            pltpu.SemaphoreType.DMA((SLOTS, 2, 2)),
            pltpu.SemaphoreType.DMA((2,)),
            pltpu.SemaphoreType.DMA((2,)),
            pltpu.SemaphoreType.REGULAR((2,)),
        ],
        compiler_params=pltpu.CompilerParams(collective_id=0, has_side_effects=True),
    )(rhs, zo.T, e_diag, a_off, e_off, col_index, inv_diag, shifts)


def solution(mesh):
    placed = (
        P("blk", "narrow"),
        P("blk", None),
        P("blk", None, None),
        P("blk", None, None, None),
        P("blk", None, None, None),
        P("blk", None),
        P(None, "blk", None, None),
        P(),
    )
    return jax.shard_map(
        functools.partial(shards, mesh.shape["blk"], mesh.shape["narrow"]),
        mesh=mesh,
        in_specs=placed,
        out_specs=(P("blk", "narrow"), P(("blk", "narrow"), None, None)),
        check_vma=False,
    )
```

```python
import functools

import jax
import jax.numpy as jnp
from jax import lax
from jax.experimental import pallas as pl
from jax.experimental.pallas import tpu as pltpu
from jax.sharding import PartitionSpec as P

SWEEPS = 8
SLOTS = 2 * (SWEEPS + 1)
OFFSETS = (-2, -1, 1, 2)
LANES = 128
E_MATRIX = 2
f32, bf16 = jnp.float32, jnp.bfloat16
NEAR, FAR = 0, 1
EDGE, INNER = 0, 1


def split(x):
    high = x.astype(bf16)
    return high, (x - high.astype(f32)).astype(bf16)


def beside(x):
    return jnp.concatenate(split(x), axis=1)


def below(x):
    return jnp.concatenate(split(x), axis=0)


def product(matrix, field):
    whole = jnp.dot(matrix, field, preferred_element_type=f32)
    rows, cols = whole.shape[0] // 2, whole.shape[1] // 2
    return (whole[:rows, :cols] + whole[:rows, cols:]) + (whole[rows:, :cols] + whole[rows:, cols:])


def kernel(
    count, others, size,
    rhs_hbm, zo_hbm, e_diag_hbm, a_off_hbm, e_off_hbm, col_ref, inv_hbm, shift_ref,
    res_ref, cross_ref,
    own, halo, pend, base, image, band, diag, local_m, halo_m, inverse, zot, partial, outbox, inbox,
    send_sem, recv_sem, cross_send, cross_recv, tokens,
    rhs_ref, zo_ref, e_diag_ref, a_off_ref, e_off_ref, inv_ref, load_sem,
):
    me = lax.axis_index("blk")
    mine = lax.axis_index("narrow")
    devices = count * others
    rank = me * others + mine
    parity = lax.rem(me, 2)
    halves = (1 - parity, parity)
    step_to = 1 - 2 * parity
    has_far = jnp.logical_and(me != 0, me != count - 1)
    near_id = me + step_to
    far_id = jnp.where(has_far, me - step_to, near_id)
    per = outbox.shape[2]

    loads = [
        pltpu.make_async_copy(source, target, load_sem.at[k])
        for k, (source, target) in enumerate((
            (rhs_hbm, rhs_ref), (inv_hbm, inv_ref), (a_off_hbm, a_off_ref), (e_off_hbm, e_off_ref),
            (e_diag_hbm, e_diag_ref), (zo_hbm, zo_ref),
        ))
    ]
    barrier = pltpu.get_barrier_semaphore()
    for load in loads:
        load.start()

    short = count <= SLOTS - 1

    def greet(**where):
        pl.semaphore_signal(barrier, inc=1, device_id=where, device_id_type=pl.DeviceIdType.MESH)

    def everyone(act):
        def at(k, carry):
            b = lax.rem(k + me + count // 2, count)
            for n in range(others):
                @pl.when(jnp.logical_or(b != me, n != mine))
                def _():
                    act(b, n)
            return carry
        lax.fori_loop(0, count, at, 0)

    if short:
        greet(blk=near_id)

        @pl.when(has_far)
        def _():
            greet(blk=far_id)

        for k in range(1, others):
            greet(narrow=lax.rem(mine + k, others))
        greeted = others + jnp.where(has_far, 1, 0)
    else:
        everyone(lambda b, n: greet(blk=b, narrow=n))
        greeted = devices - 1

    @pl.when(jnp.logical_not(has_far))
    def _():
        def clear(s, carry):
            halo[s, FAR] = jnp.zeros((2, size, LANES), f32)
            return carry
        lax.fori_loop(0, SLOTS, clear, 0)

    def block_of(side, piece):
        return 3 * halves[side] if piece == EDGE else 1 + halves[side]

    def copy_of(slot, side, piece):
        return pltpu.make_async_remote_copy(
            src_ref=own.at[slot, block_of(side, piece)],
            dst_ref=halo.at[slot, side, piece],
            send_sem=send_sem.at[slot, side, piece],
            recv_sem=recv_sem.at[slot, side, piece],
            device_id={"blk": near_id if side == NEAR else far_id},
            device_id_type=pl.DeviceIdType.MESH,
        )

    def where_linked(side, act):
        if side == NEAR:
            act()
        else:
            pl.when(has_far)(act)

    def send(slot, side, piece):
        where_linked(side, lambda: copy_of(slot, side, piece).start())

    def arrive(slot, side, piece):
        where_linked(side, lambda: copy_of(slot, side, piece).wait_recv())

    filler = jnp.zeros((LANES - size, 2 * LANES), bf16)

    def field(blocks):
        parts = []
        for block in blocks:
            parts += [beside(block), filler]
        return jnp.concatenate(parts, axis=0)

    def solved(which, block, value):
        return product(inverse[which, block], beside(value))

    def place(which, row, blocks):
        empty = jnp.zeros((size, LANES), bf16)
        half = row // 2
        for c in range(-2, 6):
            high, low = split(blocks[c - row]) if c - row in blocks else (empty, empty)
            if 0 <= c < 4:
                lanes = slice(c * LANES, (c + 1) * LANES)
                local_m[which, row * size:(row + 1) * size, lanes] = high
                local_m[which, (4 + row) * size:(5 + row) * size, lanes] = low
            elif (c < 0) == (half == 0):
                k = EDGE if c in (-1, 4) else INNER
                at = EDGE if row in (0, 3) else INNER
                lanes = slice(k * LANES, (k + 1) * LANES)
                halo_m[which, half, 2 * at * size:(2 * at + 1) * size, lanes] = high
                halo_m[which, half, (2 * at + 1) * size:(2 * at + 2) * size, lanes] = low

    def build_bands():
        band[...] = jnp.zeros_like(band)
        diag[...] = jnp.zeros_like(diag)
        for i in range(4):
            diag[i, :, 0:size] = e_diag_ref[i]
            for k, offset in enumerate(OFFSETS):
                total_a = jnp.zeros((size, size), f32)
                total_e = jnp.zeros((size, size), f32)
                for s in range(3):
                    weight = jnp.where(col_ref[i, s] == me * 4 + (i + offset), f32(1.0), f32(0.0))
                    total_a = total_a + weight * a_off_ref[i, s]
                    total_e = total_e + weight * e_off_ref[i, s]
                band[0, i, :, k * LANES:k * LANES + size] = total_a
                band[1, i, :, k * LANES:k * LANES + size] = total_e

    def build_sweep(which):
        q = shift_ref[which]
        for i in range(4):
            merged = product(inverse[which, i], beside(band[0, i] - q * band[1, i]))
            place(which, i, {o: merged[:, k * LANES:(k + 1) * LANES] for k, o in enumerate(OFFSETS)})

    def build_mass():
        for i in range(4):
            blocks = {o: band[1, i, :, k * LANES:(k + 1) * LANES] for k, o in enumerate(OFFSETS)}
            blocks[0] = diag[i]
            place(E_MATRIX, i, blocks)

    def inner(which, slot):
        return product(local_m[which], field([own[slot, b] for b in range(4)]))

    def outer(which, slot, side, emit):
        part = 2 * size
        arrive(slot, side, EDGE)
        nearest = field([halo[slot, side, EDGE]])
        matrix = halo_m.at[which, halves[side]]
        emit(block_of(side, INNER), INNER, product(matrix[part:2 * part, 0:LANES], nearest))
        edge = product(matrix[0:part, 0:LANES], nearest)
        arrive(slot, side, INNER)
        edge = edge + product(matrix[0:part, LANES:2 * LANES], field([halo[slot, side, INNER]]))
        emit(block_of(side, EDGE), EDGE, edge)

    def pass_token(token, turn, target, slot):
        @pl.when(jnp.logical_and(turn == slot, turn > 0))
        def _():
            pl.semaphore_wait(tokens.at[token], 1)

        @pl.when(jnp.logical_and(turn == slot, turn < count - 1))
        def _():
            pl.semaphore_signal(
                tokens.at[token], inc=1, device_id={"blk": target}, device_id_type=pl.DeviceIdType.MESH
            )

    def pass_tokens(slot):
        if short:
            pass_token(0, me, jnp.minimum(me + 1, count - 1), slot)
            pass_token(1, count - 1 - me, jnp.maximum(me - 1, 0), slot)

    def sweep_inner(which, slot):
        pass_tokens(slot)
        got = inner(which, slot)
        for b in range(4):
            pend[b] = base[b] - got[b * size:(b + 1) * size]

    def sweep_outer(which, slot):
        for side in (NEAR, FAR):
            def emit(block, piece, value):
                own[slot + 1, block] = pend[block] - value
                send(slot + 1, side, piece)

            outer(which, slot, side, emit)

    loads[0].wait()
    loads[1].wait()
    for i in range(4):
        inverse[0, i] = below(inv_ref[0, i])
    for b in range(4):
        start = solved(0, b, rhs_ref[b * size:(b + 1) * size])
        base[b] = start
        own[0, b] = start
    pl.semaphore_wait(barrier, greeted)
    for side in (FAR, NEAR):
        for piece in (EDGE, INNER):
            send(0, side, piece)
    for load in loads[2:]:
        load.wait()
    build_bands()
    build_sweep(0)
    for i in range(4):
        inverse[1, i] = below(inv_ref[1, i])

    def post(which):
        def act(b, n):
            pltpu.make_async_remote_copy(
                src_ref=outbox.at[which, b * others + n],
                dst_ref=inbox.at[which, rank],
                send_sem=cross_send.at[which],
                recv_sem=cross_recv.at[which],
                device_id={"blk": b, "narrow": n},
                device_id_type=pl.DeviceIdType.MESH,
            ).start()

        everyone(act)

    for which in range(2):
        first = which * (SWEEPS + 1)
        q = shift_ref[which]
        sweep_inner(which, first)
        sweep_outer(which, first)
        done = 1
        if which == 0:
            sweep_inner(which, first + 1)
            build_mass()
            sweep_outer(which, first + 1)
            sweep_inner(which, first + 2)
            build_sweep(1)
            sweep_outer(which, first + 2)
            zot[...] = below(zo_ref[...])
            done = 3

        def sweep(s, carry):
            sweep_inner(which, first + s)
            sweep_outer(which, first + s)
            return carry

        lax.fori_loop(done, SWEEPS - which, sweep, 0)
        if which == 1:
            sweep_inner(which, first + SWEEPS - 1)
            post(0)
            sweep_outer(which, first + SWEEPS - 1)

        last = first + SWEEPS
        if which == 0:
            pass_tokens(last)
        got = inner(E_MATRIX, last)
        for b in range(4):
            pend[b] = got[b * size:(b + 1) * size]
        root = jnp.sqrt(jnp.full((1, LANES), 2.0 * q, f32))
        for side in (NEAR, FAR):
            def emit(block, piece, value):
                mass = pend[block] + value
                rows = pl.ds(pl.multiple_of(block * size, 8), size)
                before = rhs_ref[rows, :] if which == 0 else res_ref[rows, :]
                after = before + (2.0 * q) * mass
                res_ref[rows, :] = after
                image[block] = root * mass
                if which == 0:
                    start = solved(1, block, after)
                    base[block] = start
                    own[last + 1, block] = start
                    send(last + 1, side, piece)

            outer(E_MATRIX, last, side, emit)

        partial[...] = product(zot[...], jnp.concatenate([beside(image[b]) for b in range(4)], axis=0))

        def pack(d, carry):
            outbox[which, d] = partial[pl.ds(d * per, per), :]
            return carry

        lax.fori_loop(0, devices, pack, 0, unroll=8)

        if which == 1:
            post(1)
        inbox[which, rank] = outbox[which, rank]

    for which in range(2):
        most = pl.ds(0, devices - 1)
        pltpu.make_async_copy(outbox.at[which, most], inbox.at[which, most], cross_recv.at[which]).wait()
        for n in range(others):
            total = inbox[which, n]
            for b in range(1, count):
                total = total + inbox[which, b * others + n]
            cross_ref[:, which, n * LANES:(n + 1) * LANES] = total
        pltpu.make_async_copy(outbox.at[which, most], inbox.at[which, most], cross_send.at[which]).wait()

    def settle(slot, carry):
        for side in (NEAR, FAR):
            for piece in (EDGE, INNER):
                where_linked(side, lambda: copy_of(slot, side, piece).wait_send())
        return carry

    lax.fori_loop(0, SLOTS, settle, 0)


def shards(count, others, rhs, zo, e_diag, a_off, e_off, col_index, inv_diag, shifts):
    row_count, col_width = rhs.shape
    size = e_diag.shape[1]
    ko = zo.shape[1]
    devices = count * others
    per = ko // devices
    assert row_count == 4 * size and col_width == LANES and count % 2 == 0
    vmem = pl.BlockSpec(memory_space=pltpu.VMEM)
    smem = pl.BlockSpec(memory_space=pltpu.SMEM)
    hbm = pl.BlockSpec(memory_space=pl.ANY)
    return pl.pallas_call(
        functools.partial(kernel, count, others, size),
        out_shape=(
            jax.ShapeDtypeStruct((row_count, col_width), f32),
            jax.ShapeDtypeStruct((per, 2, others * LANES), f32),
        ),
        in_specs=[hbm, hbm, hbm, hbm, hbm, smem, hbm, smem],
        out_specs=(vmem, vmem),
        scratch_shapes=[
            pltpu.VMEM((SLOTS, 4, size, LANES), f32),
            pltpu.VMEM((SLOTS, 2, 2, size, LANES), f32),
            pltpu.VMEM((4, size, LANES), f32),
            pltpu.VMEM((4, size, LANES), f32),
            pltpu.VMEM((4, size, LANES), f32),
            pltpu.VMEM((2, 4, size, 4 * LANES), f32),
            pltpu.VMEM((4, size, LANES), f32),
            pltpu.VMEM((3, 8 * size, 4 * LANES), bf16),
            pltpu.VMEM((3, 2, 4 * size, 2 * LANES), bf16),
            pltpu.VMEM((2, 4, 2 * size, size), bf16),
            pltpu.VMEM((2 * ko, row_count), bf16),
            pltpu.VMEM((ko, LANES), f32),
            pltpu.VMEM((2, devices, per, LANES), f32),
            pltpu.VMEM((2, devices, per, LANES), f32),
            pltpu.SemaphoreType.DMA((SLOTS, 2, 2)),
            pltpu.SemaphoreType.DMA((SLOTS, 2, 2)),
            pltpu.SemaphoreType.DMA((2,)),
            pltpu.SemaphoreType.DMA((2,)),
            pltpu.SemaphoreType.REGULAR((2,)),
            *(pltpu.VMEM(x.shape, f32) for x in (rhs, zo.T, e_diag, a_off, e_off, inv_diag)),
            pltpu.SemaphoreType.DMA((6,)),
        ],
        compiler_params=pltpu.CompilerParams(collective_id=0, has_side_effects=True),
    )(rhs, zo.T, e_diag, a_off, e_off, col_index, inv_diag, shifts)


def solution(mesh):
    placed = (
        P("blk", "narrow"),
        P("blk", None),
        P("blk", None, None),
        P("blk", None, None, None),
        P("blk", None, None, None),
        P("blk", None),
        P(None, "blk", None, None),
        P(),
    )
    return jax.shard_map(
        functools.partial(shards, mesh.shape["blk"], mesh.shape["narrow"]),
        mesh=mesh,
        in_specs=placed,
        out_specs=(P("blk", "narrow"), P(("blk", "narrow"), None, None)),
        check_vma=False,
    )
```
